32 devices in a mesh: groups: 2 (over x), particle: 8 (over z, y), classes: 2 (over core).
Axes of the slice: x: 2, y: 2, z: 4, core: 2. Of those that a mesh axis runs over, the one named last changes fastest.
Arguments:
- boxes: bfloat16 [2048, 12288], P(('groups', 'particle', 'classes')), parts along dimension 0
- counts: int32 [32], P(('groups', 'particle', 'classes')), parts along dimension 0, may hold values from 1 to 64, as said below
- destinations: int32 [2048], P(('groups', 'particle', 'classes')), parts along dimension 0, may hold values from 0 to 7, as said below
- prior_rot: int32 [2048], P(('groups', 'particle', 'classes')), parts along dimension 0, may hold values from 0 to 23
- references: bfloat16 [128, 12288], P(('groups', 'classes')), parts along dimension 0
- cycle_weights: float32 [16, 64], P(('groups', 'particle')), parts along dimension 0, may hold values from 0.01 to 0.05
- prior_strength: float32 [128], P(('groups', 'classes')), parts along dimension 0, may hold values from 0.5 to 3
Outputs:
- new_references: float32 [128, 64, 192], P(('groups', 'classes'), 'particle'), parts along dimension 0
- log_evidence: float32 [2048], P(('groups', 'particle', 'classes')), parts along dimension 0
The draws below stay inside these ranges and needn't reach their ends.
There are 2 independent parts, one for each index of `groups`. The reference program is written for one: setup_inputs(seed, part) draws one part's arguments, and reference() takes and returns one part's arrays. A program takes and returns all parts, laid end to end along the dimension named above; each array names one. Nothing has to cross between parts.
Inputs may be any that keep to these rules, and one draw needn't show every extreme that they name: On each index of classes, the counts of the 8 owners with that index sum to 128, and one of them is exactly 64. `destinations`: only an owner's first counts slots are picked; its other slots hold arbitrary indices. Each device receives exactly 16 picked boxes, all from owners with its own index of classes, and at most 8 from any one owner; some owner sends exactly 8 to one device.
All inputs are finite; a program needn't handle non-finite values.
Results may differ from the reference program's by a relative error of at most 0.004.
Values may be sent and summed in bfloat16 or wider, within the bound.
A program may use at most 192 MiB of HBM per device.

```python
import math
import jax
import jax.numpy as jnp
from jax import lax

CYCLES = 64
ANGLES = 192
CLASSES = 64
ROTATIONS = 24
REC = 16
OWN = 64
BOXES = 1024
LIVE = 256
N_PARTICLE = 8
N_CLASSES = 2


def pick_plan(key):
    plan_key = jax.random.fold_in(key, 301)
    key_full, key_share, key_rank, key_perm, key_junk = jax.random.split(plan_key, 5)
    lane_ids = jnp.arange(N_PARTICLE, dtype=jnp.int32)
    full_owner = jax.random.randint(key_full, (N_CLASSES,), 0, N_PARTICLE)
    is_full = lane_ids[None, :] == full_owner[:, None]
    shares = jnp.where(is_full, 0, jax.random.randint(key_share, (N_CLASSES, N_PARTICLE), 1, 3))
    spare = (N_PARTICLE - 4) * REC - (N_PARTICLE - 1)
    portion = spare * shares // jnp.sum(shares, axis=1, keepdims=True)
    leftover = spare - jnp.sum(portion, axis=1, keepdims=True)
    rank_keys = jax.random.randint(key_rank, (N_CLASSES, N_PARTICLE), 0, 1 << 20) * N_PARTICLE + lane_ids[None, :]
    rank_keys = jnp.where(is_full, jnp.int32(1 << 30), rank_keys)
    ranks = jnp.argsort(jnp.argsort(rank_keys, axis=1), axis=1)
    owner_counts = jnp.where(is_full, 4 * REC, 1 + portion + (ranks < leftover).astype(jnp.int32))
    positions = (lane_ids[None, :] - full_owner[:, None]) % N_PARTICLE
    earlier = positions[:, None, :] < positions[:, :, None]
    starts = jnp.sum(jnp.where(earlier, owner_counts[:, None, :], 0), axis=2)
    perms = jax.vmap(lambda sub_key: jax.random.permutation(sub_key, N_PARTICLE))(jax.random.split(key_perm, N_CLASSES))
    slot_ids = jnp.arange(OWN, dtype=jnp.int32)
    blocks = (starts[:, :, None] + slot_ids[None, None, :]) // 2 % N_PARTICLE
    routed = jnp.take_along_axis(jnp.broadcast_to(perms[:, None, :], (N_CLASSES, N_PARTICLE, N_PARTICLE)), blocks, axis=2)
    junk = jax.random.randint(key_junk, (N_CLASSES, N_PARTICLE, OWN), 0, N_PARTICLE)
    chosen = jnp.where(slot_ids[None, None, :] < owner_counts[:, :, None], routed, junk)
    dest_out = jnp.transpose(chosen, (1, 0, 2)).reshape(BOXES).astype(jnp.int32)
    count_out = jnp.transpose(owner_counts).reshape(N_PARTICLE * N_CLASSES).astype(jnp.int32)
    return (dest_out, count_out)


def base_refs(key):
    ref_key = jax.random.fold_in(key, 17)
    ref_values = jax.random.normal(ref_key, (CLASSES, CYCLES * ANGLES), jnp.float32)
    return ref_values


def draw_counts(key, part):
    return pick_plan(key)[1]


def draw_destinations(key, part):
    return pick_plan(key)[0]


def draw_references(key, part):
    return base_refs(key).astype(jnp.bfloat16)


def draw_boxes(key, part):
    box_key = jax.random.fold_in(key, 23)
    base_noise = jax.random.normal(box_key, (BOXES, CYCLES * ANGLES), jnp.float32)
    return base_noise.astype(jnp.bfloat16)


def set_ends(values, stream_key, low, high):
    dims = values.shape
    spot = [jax.random.randint(jax.random.fold_in(stream_key, axis), (), 0, dims[axis]) for axis in range(len(dims))]
    values = values.at[tuple(spot)].set(low)
    longest = dims.index(max(dims))
    spot[longest] = (spot[longest] + 1) % dims[longest]
    return values.at[tuple(spot)].set(high)


def steps_of(key, extent, shards, least, largest):
    level = 1.0
    for dim, shards_of in shards:
        steps = jax.random.uniform(jax.random.fold_in(jax.random.fold_in(key, 6), dim), (shards_of,), jnp.float32, least / len(shards), largest / len(shards))
        level = level * jnp.repeat(jnp.exp(steps), extent[dim] // shards_of).reshape((-1,) + (1,) * (len(extent) - 1 - dim))
    return level


def setup_inputs(seed: int = 0, part: int = 0) -> dict:
    keys = jax.random.split(jax.random.key(seed), 8)
    part_splits = jax.random.split(jax.random.fold_in(keys[7], part), 8)
    return {
        "boxes": draw_boxes(jax.random.fold_in(jax.random.fold_in(keys[7], part), 71), part),
        "counts": draw_counts(jax.random.fold_in(jax.random.fold_in(keys[7], part), 71), part),
        "destinations": draw_destinations(jax.random.fold_in(jax.random.fold_in(keys[7], part), 71), part),
        "prior_rot": set_ends(jax.random.randint(part_splits[3], (BOXES,), 0, ROTATIONS), jax.random.fold_in(part_splits[3], 1), 0, ROTATIONS - 1).astype(jnp.int32),
        "references": draw_references(jax.random.fold_in(jax.random.fold_in(keys[7], part), 71), part),
        "cycle_weights": jnp.clip(jnp.exp(math.log(0.05) - 1.609438 * jax.random.uniform(part_splits[5], (N_PARTICLE, CYCLES), jnp.float32) ** steps_of(part_splits[5], (N_PARTICLE, CYCLES), ((0, 8),), -0.2, 0.2)), 0.01, 0.05),
        "prior_strength": jnp.clip(jnp.exp(math.log(3.0) - 1.7917595 * jax.random.uniform(part_splits[6], (CLASSES,), jnp.float32) ** steps_of(part_splits[6], (CLASSES,), ((0, 2),), -0.2, 0.2)), 0.5, 3.0),
    }


HIGHEST = lax.Precision.HIGHEST
TWO_PI = 2.0 * math.pi


def rotated_stack(ref_cube, turn_shift):
    return jnp.concatenate([jnp.roll(ref_cube, turn_id * turn_shift, axis=2) for turn_id in range(ROTATIONS)], axis=0)


def score_rows(box_rows, row_wts, prior_turn, ref_stack, energy, strength):
    cycle_dots = jnp.einsum("nga,qga->gnq", box_rows.astype(jnp.float32), ref_stack.astype(jnp.float32), precision=HIGHEST)
    weighted = jnp.einsum("gnq,ng->nq", cycle_dots, row_wts, precision=HIGHEST)
    row_count = box_rows.shape[0]
    class_count = energy.shape[0]
    weighted = weighted.reshape(row_count, ROTATIONS, class_count)
    offset = -0.5 * jnp.dot(row_wts, energy.T, precision=HIGHEST)
    turn_ids = jnp.arange(ROTATIONS, dtype=jnp.float32)
    angle_gap = TWO_PI * (turn_ids[None, :] - prior_turn[:, None].astype(jnp.float32)) / ROTATIONS
    return weighted + offset[:, None, :] + jnp.cos(angle_gap)[:, :, None] * strength[None, None, :]


def reference(boxes, counts, destinations, prior_rot, references, cycle_weights, prior_strength):
    turn_shift = ANGLES // ROTATIONS
    slot_ids = jnp.arange(BOXES, dtype=jnp.int32)
    is_live = (slot_ids % OWN) < jnp.repeat(counts, OWN, total_repeat_length=BOXES)
    picked = jnp.nonzero(is_live, size=LIVE)[0].astype(jnp.int32)
    box_rows = boxes[picked].reshape(LIVE, CYCLES, ANGLES)
    row_wts = cycle_weights[destinations[picked]]
    prior_turn = prior_rot[picked].astype(jnp.float32)
    ref_cube = references.reshape(CLASSES, CYCLES, ANGLES)
    ref_stack = rotated_stack(ref_cube, turn_shift)
    ref_wide = ref_cube.astype(jnp.float32)
    energy = jnp.sum(ref_wide * ref_wide, axis=2)
    block_rows = math.gcd(LIVE, 64)

    def one_block(block_id):
        first_row = block_id * block_rows
        return score_rows(lax.dynamic_slice_in_dim(box_rows, first_row, block_rows, 0),
                          lax.dynamic_slice_in_dim(row_wts, first_row, block_rows, 0),
                          lax.dynamic_slice_in_dim(prior_turn, first_row, block_rows, 0),
                          ref_stack, energy, prior_strength)

    scores = lax.map(one_block, jnp.arange(LIVE // block_rows, dtype=jnp.int32)).reshape(LIVE, ROTATIONS, CLASSES)
    row_top = jnp.max(scores, axis=(1, 2))
    exp_terms = jnp.exp(scores - row_top[:, None, None])
    norm_sum = jnp.sum(exp_terms, axis=(1, 2))
    weights = (exp_terms / norm_sum[:, None, None]).astype(jnp.bfloat16)
    evidence_live = (row_top + jnp.log(norm_sum)) / (ANGLES * jnp.sum(row_wts, axis=1))
    evidence = jnp.zeros((BOXES,), jnp.float32).at[picked].set(evidence_live)
    class_sum = jnp.zeros((CLASSES, CYCLES, ANGLES), jnp.float32)
    for turn_id in range(ROTATIONS):
        spread = jnp.einsum("nk,nga->kga", weights[:, turn_id, :].astype(jnp.float32), box_rows.astype(jnp.float32), precision=HIGHEST)
        class_sum = class_sum + jnp.roll(spread, -turn_id * turn_shift, axis=2)
    class_mass = jnp.sum(weights.astype(jnp.float32), axis=(0, 1))
    new_references = (class_sum + ref_wide) / (class_mass + 1.0)[:, None, None]
    return new_references, evidence
```

```python
import functools
import math

import jax
import jax.numpy as jnp
from jax import lax
from jax.experimental import pallas as pl
from jax.experimental.pallas import tpu as pltpu
from jax.sharding import PartitionSpec as P

CYCLES = 64
ANGLES = 192
ROTATIONS = 24
FINE = 4
COARSE = ROTATIONS // FINE
SHIFT = ANGLES // ROTATIONS
STEP_CYCLES = 4
STEP = STEP_CYCLES * ANGLES
STEPS = CYCLES // STEP_CYCLES
TWO_PI = 2.0 * math.pi


def roll_rows(block, shift):
    shift = shift % ANGLES
    if shift == 0:
        return block
    pieces = []
    for c in range(STEP_CYCLES):
        base = c * ANGLES
        pieces.append(block[base + ANGLES - shift : base + ANGLES])
        pieces.append(block[base : base + ANGLES - shift])
    return jnp.concatenate(pieces, axis=0)


def fan_out(rows, sign):
    plain = jnp.concatenate([rows, rows], axis=0).T
    low = lax.broadcasted_iota(jnp.int32, plain.shape, 1) < rows.shape[0]
    tiles = [
        jnp.where(low, roll_rows(plain, sign * SHIFT * f), roll_rows(plain, sign * SHIFT * (f + 1)))
        for f in range(0, FINE, 2)
    ]
    return jnp.concatenate([t.astype(jnp.bfloat16) for t in tiles], axis=1), plain


def kernel(cycles_dev, boxes_ref, refs_ref, wts_ref, aux_ref, str_ref, out_ref, ev_ref,
           acc, off, post, mass):
    phase, step = pl.program_id(0), pl.program_id(1)
    owned = boxes_ref.shape[0]
    half = str_ref.shape[1]

    @pl.when((phase == 0) & (step == 0))
    def _():
        acc[...] = jnp.zeros_like(acc)
        off[...] = jnp.zeros_like(off)

    @pl.when(phase == 0)
    def _():
        wts = wts_ref[0]
        lane = lax.broadcasted_iota(jnp.int32, (owned, STEP), 1)
        spread = jnp.broadcast_to(wts[:, 0:1], (owned, STEP))
        for c in range(1, STEP_CYCLES):
            spread = jnp.where(lane >= c * ANGLES, wts[:, c : c + 1], spread)
        scaled = boxes_ref[...].astype(jnp.float32) * spread
        high = scaled.astype(jnp.bfloat16)
        rest = (scaled - high.astype(jnp.float32)).astype(jnp.bfloat16)
        lhs = jnp.concatenate([high, rest], axis=0)
        fan, plain = fan_out(refs_ref[...].astype(jnp.float32), 1)
        total = off[...]
        for c in range(STEP_CYCLES):
            piece = plain[c * ANGLES : (c + 1) * ANGLES]
            total = total + wts[:, c : c + 1] * jnp.sum(piece * piece, axis=0, keepdims=True)
        off[...] = total
        for q in range(COARSE):
            acc[q] += jnp.dot(
                lhs, roll_rows(fan, SHIFT * FINE * q), preferred_element_type=jnp.float32
            )

    @pl.when((phase == 0) & (step == STEPS - 1))
    def _():
        aux = aux_ref[...]
        live = aux[:, ROTATIONS : ROTATIONS + 1]
        wsum = aux[:, ROTATIONS + 1 : ROTATIONS + 2]
        low = lax.broadcasted_iota(jnp.int32, (owned, half), 1) < owned
        base = -0.5 * off[...]
        strength = str_ref[...]
        top = None
        for q in range(COARSE):
            for t in range(FINE // 2):
                r = q * FINE + 2 * t
                cols = slice(t * half, (t + 1) * half)
                turn = jnp.where(low, aux[:, r : r + 1], aux[:, r + 1 : r + 2])
                score = acc[q, :owned, cols] + acc[q, owned:, cols] + base + turn * strength
                acc[q, :owned, cols] = score
                top = score if top is None else jnp.maximum(top, score)
        top = jnp.max(top, axis=1, keepdims=True)
        norm = jnp.zeros((owned, half), jnp.float32)
        for q in range(COARSE):
            for t in range(FINE // 2):
                cols = slice(t * half, (t + 1) * half)
                term = jnp.exp(acc[q, :owned, cols] - top)
                acc[q, :owned, cols] = term
                norm = norm + term
        norm = jnp.sum(norm, axis=1, keepdims=True)
        ev_ref[...] = jnp.where(live > 0.0, (top + jnp.log(norm)) / (ANGLES * wsum), 0.0)
        seen = jnp.zeros((owned, half), jnp.float32)

        def weight(q, t):
            cols = slice(t * half, (t + 1) * half)
            value = jnp.where(live > 0.0, acc[q, :owned, cols] / norm, 0.0)
            return value.astype(jnp.bfloat16).astype(jnp.float32)

        for q in range(0, COARSE, 2):
            for t in range(FINE // 2):
                first, second = weight(q, t), weight(q + 1, t)
                seen = seen + first + second
                even = jnp.where(low, first, pltpu.roll(second, half // 2, 1))
                odd = jnp.where(low, pltpu.roll(first, half // 2, 1), second)
                cols = slice(q // 2 * half, (q // 2 + 1) * half)
                post[2 * t * owned : (2 * t + 1) * owned, cols] = even.astype(jnp.bfloat16)
                post[(2 * t + 1) * owned : (2 * t + 2) * owned, cols] = odd.astype(jnp.bfloat16)
        seen = jnp.sum(seen, axis=0, keepdims=True)
        seen = jnp.broadcast_to(seen, (half, half))
        seen = seen + pltpu.roll(seen, half // 2, 1)
        mass[...] = seen.T

    @pl.when(phase == 1)
    def _():
        fan, _unused = fan_out(boxes_ref[...].astype(jnp.float32), -1)
        sums = jnp.dot(fan, post[...], preferred_element_type=jnp.float32)
        both = sums[:, :half]
        for p in range(1, COARSE // 2):
            both = both + roll_rows(sums[:, p * half : (p + 1) * half], -2 * p * SHIFT * FINE)
        whole = both + pltpu.roll(roll_rows(both, -SHIFT * FINE), half // 2, 1)
        turned = whole.T
        classes = half // 4
        width = cycles_dev * ANGLES
        for h in range(2):
            rows = turned[h * classes : (h + 1) * classes]
            tail = mass[h * classes : (h + 1) * classes, :]
            if width >= STEP:
                start = pl.multiple_of(step % (width // STEP) * STEP, 128)
                out_ref[0, h, :, pl.ds(start, STEP)] = rows
                out_ref[0, h, :, width:] = tail[:, : out_ref.shape[3] - width]
            else:
                for j in range(STEP // width):
                    out_ref[j, h, :, :width] = rows[:, j * width : (j + 1) * width]
                    out_ref[j, h, :, width:] = tail[:, : out_ref.shape[3] - width]


def class_terms(boxes, refs, wts, aux, strength, peers):
    cycles_dev = CYCLES // peers
    width = cycles_dev * ANGLES
    padded = (width + 1 + 127) // 128 * 128
    owned = boxes.shape[0]
    classes = refs.shape[0]
    half = 2 * classes
    if width >= STEP:
        per = width // STEP
        out_spec = pl.BlockSpec((1, 2, classes // 2, padded), lambda p, i: (p * (i // per), 0, 0, 0))
    else:
        out_spec = pl.BlockSpec(
            (STEP // width, 2, classes // 2, padded), lambda p, i: (p * i, 0, 0, 0)
        )
    hold = lambda p, i: i * (1 - p) + (STEPS - 1) * p
    return pl.pallas_call(
        functools.partial(kernel, cycles_dev),
        grid=(2, STEPS),
        in_specs=[
            pl.BlockSpec((owned, STEP), lambda p, i: (0, i)),
            pl.BlockSpec((classes, STEP), lambda p, i: (0, hold(p, i))),
            pl.BlockSpec((1, owned, STEP_CYCLES), lambda p, i: (hold(p, i), 0, 0)),
            pl.BlockSpec(aux.shape, lambda p, i: (0, 0)),
            pl.BlockSpec((1, half), lambda p, i: (0, 0)),
        ],
        out_specs=[out_spec, pl.BlockSpec((owned, 1), lambda p, i: (0, 0))],
        out_shape=[
            jax.ShapeDtypeStruct((peers, 2, classes // 2, padded), jnp.float32),
            jax.ShapeDtypeStruct((owned, 1), jnp.float32),
        ],
        scratch_shapes=[
            pltpu.VMEM((COARSE, 2 * owned, FINE * classes), jnp.float32),
            pltpu.VMEM((owned, half), jnp.float32),
            pltpu.VMEM((FINE * owned, COARSE * classes), jnp.bfloat16),
            pltpu.VMEM((half, half), jnp.float32),
        ],
        compiler_params=pltpu.CompilerParams(
            dimension_semantics=("arbitrary", "arbitrary"), vmem_limit_bytes=40 * 1024 * 1024
        ),
    )(boxes, refs, wts, aux, strength)


def on_device(boxes, counts, destinations, prior_rot, references, cycle_weights, prior_strength):
    peers = lax.axis_size("particle")
    cycle_index = lax.axis_index("particle")
    cycles_dev = CYCLES // peers
    width = cycles_dev * ANGLES
    owned = boxes.shape[0]
    refs = lax.all_gather(references, "classes", axis=0, tiled=True)
    small = lax.all_gather(
        jnp.concatenate([cycle_weights[0], prior_strength]), ("particle", "classes"), axis=0
    )
    small = small.reshape(peers, 2, -1)
    group_wts = small[:, 0, :CYCLES]
    strength = small[0, :, CYCLES:].reshape(1, -1)
    mine = destinations[:, None] == jnp.arange(peers, dtype=jnp.int32)[None, :]
    wts = jnp.sum(jnp.where(mine[:, :, None], group_wts[None], 0.0), axis=1)
    live = (jnp.arange(owned, dtype=jnp.int32) < counts[0]).astype(jnp.float32)
    turn_ids = jnp.arange(ROTATIONS, dtype=jnp.float32)
    gap = TWO_PI * (turn_ids[None, :] - prior_rot[:, None].astype(jnp.float32)) / ROTATIONS
    aux = jnp.concatenate([jnp.cos(gap), live[:, None], jnp.sum(wts, axis=1)[:, None]], axis=1)
    wts = jnp.transpose(wts.reshape(owned, STEPS, STEP_CYCLES), (1, 0, 2))
    parts, evidence = class_terms(
        boxes, refs, wts, aux, jnp.concatenate([strength, strength], axis=1), peers
    )
    classes_dev = references.shape[0]
    sums = lax.psum_scatter(
        parts.reshape(peers * 2, classes_dev, -1), ("particle", "classes"), scatter_dimension=0
    )
    own_refs = lax.dynamic_slice_in_dim(references, cycle_index * width, width, 1)
    new_references = (sums[:, :width] + own_refs.astype(jnp.float32)) / (
        sums[:, width : width + 1] + 1.0
    )
    return new_references.reshape(classes_dev, cycles_dev, ANGLES), evidence[:, 0]


def solution(mesh):
    in_specs = (
        P(("groups", "particle", "classes"), None),
        P(("groups", "particle", "classes")),
        P(("groups", "particle", "classes")),
        P(("groups", "particle", "classes")),
        P(("groups", "classes"), None),
        P(("groups", "particle"), None),
        P(("groups", "classes")),
    )
    out_specs = (P(("groups", "classes"), "particle", None), P(("groups", "particle", "classes")))
    return jax.shard_map(
        on_device, mesh=mesh, in_specs=in_specs, out_specs=out_specs, check_vma=False
    )
```

```python
import functools
import math

import jax
import jax.numpy as jnp
from jax import lax
from jax.experimental import pallas as pl
from jax.experimental.pallas import tpu as pltpu
from jax.sharding import PartitionSpec as P

CYCLES = 64
ANGLES = 192
ROTATIONS = 24
FINE = 4
COARSE = ROTATIONS // FINE
SHIFT = ANGLES // ROTATIONS
STEP_CYCLES = 4
STEP = STEP_CYCLES * ANGLES
STEPS = CYCLES // STEP_CYCLES
TWO_PI = 2.0 * math.pi


def roll_rows(block, shift):
    shift = shift % ANGLES
    if shift == 0:
        return block
    pieces = []
    for c in range(STEP_CYCLES):
        base = c * ANGLES
        pieces.append(block[base + ANGLES - shift : base + ANGLES])
        pieces.append(block[base : base + ANGLES - shift])
    return jnp.concatenate(pieces, axis=0)


def fan_out(rows, sign):
    plain = jnp.concatenate([rows, rows], axis=0).T
    low = lax.broadcasted_iota(jnp.int32, plain.shape, 1) < rows.shape[0]
    tiles = [
        jnp.where(low, roll_rows(plain, sign * SHIFT * f), roll_rows(plain, sign * SHIFT * (f + 1)))
        for f in range(0, FINE, 2)
    ]
    return jnp.concatenate([t.astype(jnp.bfloat16) for t in tiles], axis=1), plain


def kernel(cycles_dev, boxes_ref, refs_ref, wts_ref, aux_ref, str_ref, out_ref, ev_ref,
           acc, off, post, mass):
    phase, step = pl.program_id(0), pl.program_id(1)
    owned = boxes_ref.shape[0]
    half = str_ref.shape[1]

    @pl.when((phase == 0) & (step == 0))
    def _():
        acc[...] = jnp.zeros_like(acc)
        off[...] = jnp.zeros_like(off)

    @pl.when(phase == 0)
    def _():
        wts = wts_ref[0]
        lane = lax.broadcasted_iota(jnp.int32, (owned, STEP), 1)
        spread = jnp.broadcast_to(wts[:, 0:1], (owned, STEP))
        for c in range(1, STEP_CYCLES):
            spread = jnp.where(lane >= c * ANGLES, wts[:, c : c + 1], spread)
        scaled = boxes_ref[...].astype(jnp.float32) * spread
        high = scaled.astype(jnp.bfloat16)
        rest = (scaled - high.astype(jnp.float32)).astype(jnp.bfloat16)
        lhs = jnp.concatenate([high, rest], axis=0)
        fan, plain = fan_out(refs_ref[...].astype(jnp.float32), 1)
        total = off[...]
        for c in range(STEP_CYCLES):
            piece = plain[c * ANGLES : (c + 1) * ANGLES]
            total = total + wts[:, c : c + 1] * jnp.sum(piece * piece, axis=0, keepdims=True)
        off[...] = total
        for q in range(COARSE):
            acc[q] += jnp.dot(
                lhs, roll_rows(fan, SHIFT * FINE * q), preferred_element_type=jnp.float32
            )

    @pl.when((phase == 0) & (step == STEPS - 1))
    def _():
        aux = aux_ref[...]
        live = aux[:, ROTATIONS : ROTATIONS + 1]
        wsum = aux[:, ROTATIONS + 1 : ROTATIONS + 2]
        low = lax.broadcasted_iota(jnp.int32, (owned, half), 1) < owned
        base = -0.5 * off[...]
        strength = str_ref[...]
        top = None
        for q in range(COARSE):
            for t in range(FINE // 2):
                r = q * FINE + 2 * t
                cols = slice(t * half, (t + 1) * half)
                turn = jnp.where(low, aux[:, r : r + 1], aux[:, r + 1 : r + 2])
                score = acc[q, :owned, cols] + acc[q, owned:, cols] + base + turn * strength
                acc[q, :owned, cols] = score
                top = score if top is None else jnp.maximum(top, score)
        top = jnp.max(top, axis=1, keepdims=True)
        norm = jnp.zeros((owned, half), jnp.float32)
        for q in range(COARSE):
            for t in range(FINE // 2):
                cols = slice(t * half, (t + 1) * half)
                term = jnp.exp(acc[q, :owned, cols] - top)
                acc[q, :owned, cols] = term
                norm = norm + term
        norm = jnp.sum(norm, axis=1, keepdims=True)
        ev_ref[...] = jnp.where(live > 0.0, (top + jnp.log(norm)) / (ANGLES * wsum), 0.0)
        seen = jnp.zeros((owned, half), jnp.float32)

        def weight(q, t):
            cols = slice(t * half, (t + 1) * half)
            value = jnp.where(live > 0.0, acc[q, :owned, cols] / norm, 0.0)
            return value.astype(jnp.bfloat16).astype(jnp.float32)

        for q in range(0, COARSE, 2):
            for t in range(FINE // 2):
                first, second = weight(q, t), weight(q + 1, t)
                seen = seen + first + second
                even = jnp.where(low, first, pltpu.roll(second, half // 2, 1))
                odd = jnp.where(low, pltpu.roll(first, half // 2, 1), second)
                cols = slice(q // 2 * half, (q // 2 + 1) * half)
                post[2 * t * owned : (2 * t + 1) * owned, cols] = even.astype(jnp.bfloat16)
                post[(2 * t + 1) * owned : (2 * t + 2) * owned, cols] = odd.astype(jnp.bfloat16)
        seen = jnp.sum(seen, axis=0, keepdims=True)
        seen = jnp.broadcast_to(seen, (half, half))
        seen = seen + pltpu.roll(seen, half // 2, 1)
        mass[...] = seen.T

    @pl.when(phase == 1)
    def _():
        fan, _unused = fan_out(boxes_ref[...].astype(jnp.float32), -1)
        sums = jnp.dot(fan, post[...], preferred_element_type=jnp.float32)
        both = sums[:, :half]
        for p in range(1, COARSE // 2):
            both = both + roll_rows(sums[:, p * half : (p + 1) * half], -2 * p * SHIFT * FINE)
        whole = both + pltpu.roll(roll_rows(both, -SHIFT * FINE), half // 2, 1)
        turned = whole.T
        classes = half // 4
        width = cycles_dev * ANGLES
        for h in range(2):
            rows = turned[h * classes : (h + 1) * classes]
            tail = mass[h * classes : (h + 1) * classes, :]
            if width >= STEP:
                start = pl.multiple_of(step % (width // STEP) * STEP, 128)
                out_ref[0, h, :, pl.ds(start, STEP)] = rows
                out_ref[0, h, :, width:] = tail[:, : out_ref.shape[3] - width]
            else:
                for j in range(STEP // width):
                    out_ref[j, h, :, :width] = rows[:, j * width : (j + 1) * width]
                    out_ref[j, h, :, width:] = tail[:, : out_ref.shape[3] - width]


def class_terms(boxes, refs, wts, aux, strength, peers):
    cycles_dev = CYCLES // peers
    width = cycles_dev * ANGLES
    padded = (width + 1 + 127) // 128 * 128
    owned = boxes.shape[0]
    classes = refs.shape[0]
    half = 2 * classes
    if width >= STEP:
        per = width // STEP
        out_spec = pl.BlockSpec((1, 2, classes // 2, padded), lambda p, i: (p * (i // per), 0, 0, 0))
    else:
        out_spec = pl.BlockSpec(
            (STEP // width, 2, classes // 2, padded), lambda p, i: (p * i, 0, 0, 0)
        )
    hold = lambda p, i: i * (1 - p) + (STEPS - 1) * p
    return pl.pallas_call(
        functools.partial(kernel, cycles_dev),
        grid=(2, STEPS),
        in_specs=[
            pl.BlockSpec((owned, STEP), lambda p, i: (0, i)),
            pl.BlockSpec((classes, STEP), lambda p, i: (0, hold(p, i))),
            pl.BlockSpec((1, owned, STEP_CYCLES), lambda p, i: (hold(p, i), 0, 0)),
            pl.BlockSpec(aux.shape, lambda p, i: (0, 0)),
            pl.BlockSpec((1, half), lambda p, i: (0, 0)),
        ],
        out_specs=[out_spec, pl.BlockSpec((owned, 1), lambda p, i: (0, 0))],
        out_shape=[
            jax.ShapeDtypeStruct((peers, 2, classes // 2, padded), jnp.float32),
            jax.ShapeDtypeStruct((owned, 1), jnp.float32),
        ],
        scratch_shapes=[
            pltpu.VMEM((COARSE, 2 * owned, FINE * classes), jnp.float32),
            pltpu.VMEM((owned, half), jnp.float32),
            pltpu.VMEM((FINE * owned, COARSE * classes), jnp.bfloat16),
            pltpu.VMEM((half, half), jnp.float32),
        ],
        compiler_params=pltpu.CompilerParams(
            dimension_semantics=("arbitrary", "arbitrary"), vmem_limit_bytes=40 * 1024 * 1024
        ),
    )(boxes, refs, wts, aux, strength)


MESH = pl.DeviceIdType.MESH
CHUNKS = 4


def greet(devices):
    barrier = pltpu.get_barrier_semaphore()
    for device in devices:
        pl.semaphore_signal(barrier, inc=1, device_id=device, device_id_type=MESH)
    pl.semaphore_wait(barrier, len(devices))


def gather_kernel(peers, refs_ref, row_ref, all_refs, all_rows, local, send, recv):
    mine, core = lax.axis_index("particle"), lax.axis_index("classes")
    partner = {"classes": 1 - core}
    others = [{"particle": lax.rem(mine + d, peers)} for d in range(1, peers)]
    greet([partner] + others)
    copies = [
        pltpu.make_async_remote_copy(
            src_ref=refs_ref, dst_ref=all_refs.at[core], send_sem=send.at[0], recv_sem=recv.at[0],
            device_id=partner, device_id_type=MESH,
        ),
        pltpu.make_async_remote_copy(
            src_ref=row_ref, dst_ref=all_rows.at[peers], send_sem=send.at[1], recv_sem=recv.at[1],
            device_id=partner, device_id_type=MESH,
        ),
    ]
    for d, other in enumerate(others):
        copies.append(
            pltpu.make_async_remote_copy(
                src_ref=row_ref, dst_ref=all_rows.at[mine], send_sem=send.at[2 + d],
                recv_sem=recv.at[2 + d], device_id=other, device_id_type=MESH,
            )
        )
    for copy in copies:
        copy.start()
    own = [
        pltpu.make_async_copy(refs_ref, all_refs.at[core], local.at[0]),
        pltpu.make_async_copy(row_ref, all_rows.at[mine], local.at[1]),
    ]
    for copy in own:
        copy.start()
    for copy in own + copies:
        copy.wait()


def gathered(refs, row, peers):
    return pl.pallas_call(
        functools.partial(gather_kernel, peers),
        in_specs=[pl.BlockSpec(memory_space=pltpu.VMEM)] * 2,
        out_specs=[pl.BlockSpec(memory_space=pltpu.VMEM)] * 2,
        out_shape=[
            jax.ShapeDtypeStruct((2,) + refs.shape, refs.dtype),
            jax.ShapeDtypeStruct((peers + 1,) + row.shape, row.dtype),
        ],
        scratch_shapes=[
            pltpu.SemaphoreType.DMA((2,)),
            pltpu.SemaphoreType.DMA((peers + 1,)),
            pltpu.SemaphoreType.DMA((peers + 1,)),
        ],
        compiler_params=pltpu.CompilerParams(collective_id=0, has_side_effects=True),
    )(refs, row)


def scatter_kernel(depth, parts, out, pair_in, side_out, side_in, line_out, line_in,
                   pair_send, pair_recv, side_send, side_recv, line_send, line_recv):
    mine, core = lax.axis_index("particle"), lax.axis_index("classes")
    level, side = mine // 2, lax.rem(mine, 2)
    partner = {"classes": 1 - core}
    across = {"particle": level * 2 + 1 - side}
    levels = [lax.rem(level + d, depth) for d in range(1, depth)]
    line = [{"particle": other * 2 + side} for other in levels]
    greet([partner, across] + line)
    rows = out.shape[0] // CHUNKS
    pair, cross, lines = [], [], []
    for j in range(CHUNKS):
        copy = pltpu.make_async_remote_copy(
            src_ref=parts.at[:, :, 1 - core, j * rows : (j + 1) * rows], dst_ref=pair_in.at[j],
            send_sem=pair_send.at[j], recv_sem=pair_recv.at[j], device_id=partner,
            device_id_type=MESH,
        )
        copy.start()
        pair.append(copy)
    for j in range(CHUNKS):
        span = slice(j * rows, (j + 1) * rows)
        pair[j].wait_recv()
        side_out[j] = parts[:, 1 - side, core, span] + pair_in[j, :, 1 - side]
        copy = pltpu.make_async_remote_copy(
            src_ref=side_out.at[j], dst_ref=side_in.at[j], send_sem=side_send.at[j],
            recv_sem=side_recv.at[j], device_id=across, device_id_type=MESH,
        )
        copy.start()
        cross.append(copy)
        line_out[j] = parts[:, side, core, span] + pair_in[j, :, side]
    for j in range(CHUNKS):
        cross[j].wait_recv()
        line_out[j] = line_out[j] + side_in[j]
        for d in range(depth - 1):
            copy = pltpu.make_async_remote_copy(
                src_ref=line_out.at[j, levels[d]], dst_ref=line_in.at[j, d],
                send_sem=line_send.at[j, d], recv_sem=line_recv.at[j, d], device_id=line[d],
                device_id_type=MESH,
            )
            copy.start()
            lines.append(copy)
    for j in range(CHUNKS):
        total = line_out[j, level]
        for d in range(depth - 1):
            lines[j * (depth - 1) + d].wait_recv()
            total = total + line_in[j, d]
        out[j * rows : (j + 1) * rows] = total
    for copy in pair + cross + lines:
        copy.wait_send()


def scattered(parts):
    peers, _, classes, width = parts.shape
    depth = peers // 2
    rows = classes // CHUNKS
    sems = pltpu.SemaphoreType.DMA((CHUNKS,))
    line_sems = pltpu.SemaphoreType.DMA((CHUNKS, max(depth - 1, 1)))
    return pl.pallas_call(
        functools.partial(scatter_kernel, depth),
        in_specs=[pl.BlockSpec(memory_space=pltpu.VMEM)],
        out_specs=pl.BlockSpec(memory_space=pltpu.VMEM),
        out_shape=jax.ShapeDtypeStruct((classes, width), jnp.float32),
        scratch_shapes=[
            pltpu.VMEM((CHUNKS, depth, 2, rows, width), jnp.float32),
            pltpu.VMEM((CHUNKS, depth, rows, width), jnp.float32),
            pltpu.VMEM((CHUNKS, depth, rows, width), jnp.float32),
            pltpu.VMEM((CHUNKS, depth, rows, width), jnp.float32),
            pltpu.VMEM((CHUNKS, max(depth - 1, 1), rows, width), jnp.float32),
            sems, sems, sems, sems, line_sems, line_sems,
        ],
        compiler_params=pltpu.CompilerParams(
            collective_id=1, has_side_effects=True, vmem_limit_bytes=48 * 1024 * 1024
        ),
    )(parts.reshape(depth, 2, 2, classes, width))


def on_device(boxes, counts, destinations, prior_rot, references, cycle_weights, prior_strength):
    peers = lax.axis_size("particle")
    cycle_index = lax.axis_index("particle")
    cycles_dev = CYCLES // peers
    width = cycles_dev * ANGLES
    owned = boxes.shape[0]
    classes_dev = references.shape[0]
    lane_index = lax.axis_index("classes")
    row = jnp.concatenate([cycle_weights[0], prior_strength])
    row = jnp.pad(row, (0, 128 - row.shape[0]))[None, :]
    refs, rows = gathered(references, row, peers)
    refs = refs.reshape(2 * classes_dev, -1)
    group_wts = rows[:peers, 0, :CYCLES]
    other = rows[peers, 0, CYCLES : CYCLES + classes_dev]
    strength = jnp.where(
        lane_index == 0,
        jnp.concatenate([prior_strength, other]),
        jnp.concatenate([other, prior_strength]),
    ).reshape(1, -1)
    mine = destinations[:, None] == jnp.arange(peers, dtype=jnp.int32)[None, :]
    wts = jnp.sum(jnp.where(mine[:, :, None], group_wts[None], 0.0), axis=1)
    live = (jnp.arange(owned, dtype=jnp.int32) < counts[0]).astype(jnp.float32)
    turn_ids = jnp.arange(ROTATIONS, dtype=jnp.float32)
    gap = TWO_PI * (turn_ids[None, :] - prior_rot[:, None].astype(jnp.float32)) / ROTATIONS
    aux = jnp.concatenate([jnp.cos(gap), live[:, None], jnp.sum(wts, axis=1)[:, None]], axis=1)
    wts = jnp.transpose(wts.reshape(owned, STEPS, STEP_CYCLES), (1, 0, 2))
    parts, evidence = class_terms(
        boxes, refs, wts, aux, jnp.concatenate([strength, strength], axis=1), peers
    )
    sums = scattered(parts)
    own_refs = lax.dynamic_slice_in_dim(references, cycle_index * width, width, 1)
    new_references = (sums[:, :width] + own_refs.astype(jnp.float32)) / (
        sums[:, width : width + 1] + 1.0
    )
    return new_references.reshape(classes_dev, cycles_dev, ANGLES), evidence[:, 0]


def solution(mesh):
    in_specs = (
        P(("groups", "particle", "classes"), None),
        P(("groups", "particle", "classes")),
        P(("groups", "particle", "classes")),
        P(("groups", "particle", "classes")),
        P(("groups", "classes"), None),
        P(("groups", "particle"), None),
        P(("groups", "classes")),
    )
    out_specs = (P(("groups", "classes"), "particle", None), P(("groups", "particle", "classes")))
    return jax.shard_map(
        on_device, mesh=mesh, in_specs=in_specs, out_specs=out_specs, check_vma=False
    )
```

```python
import functools
import math

import jax
import jax.numpy as jnp
from jax import lax
from jax.experimental import pallas as pl
from jax.experimental.pallas import tpu as pltpu
from jax.sharding import PartitionSpec as P

CYCLES = 64
ANGLES = 192
ROTATIONS = 24
FINE = 4
COARSE = ROTATIONS // FINE
SHIFT = ANGLES // ROTATIONS
STEP_CYCLES = 4
STEP = STEP_CYCLES * ANGLES
STEPS = CYCLES // STEP_CYCLES
TWO_PI = 2.0 * math.pi


def roll_rows(block, shift):
    shift = shift % ANGLES
    if shift == 0:
        return block
    pieces = []
    for c in range(STEP_CYCLES):
        base = c * ANGLES
        pieces.append(block[base + ANGLES - shift : base + ANGLES])
        pieces.append(block[base : base + ANGLES - shift])
    return jnp.concatenate(pieces, axis=0)


def fan_out(rows, sign):
    plain = jnp.concatenate([rows, rows], axis=0).T
    low = lax.broadcasted_iota(jnp.int32, plain.shape, 1) < rows.shape[0]
    tiles = [
        jnp.where(low, roll_rows(plain, sign * SHIFT * f), roll_rows(plain, sign * SHIFT * (f + 1)))
        for f in range(0, FINE, 2)
    ]
    return jnp.concatenate([t.astype(jnp.bfloat16) for t in tiles], axis=1), plain


def score_kernel(boxes_ref, refs_ref, wts_ref, aux_ref, str_ref, post, mass, ev_ref, acc, off):
    step = pl.program_id(0)
    owned = boxes_ref.shape[0]
    half = str_ref.shape[1]

    @pl.when(step == 0)
    def _():
        acc[...] = jnp.zeros_like(acc)
        off[...] = jnp.zeros_like(off)

    @pl.when(step >= 0)
    def _():
        wts = wts_ref[0]
        lane = lax.broadcasted_iota(jnp.int32, (owned, STEP), 1)
        spread = jnp.broadcast_to(wts[:, 0:1], (owned, STEP))
        for c in range(1, STEP_CYCLES):
            spread = jnp.where(lane >= c * ANGLES, wts[:, c : c + 1], spread)
        scaled = boxes_ref[...].astype(jnp.float32) * spread
        high = scaled.astype(jnp.bfloat16)
        rest = (scaled - high.astype(jnp.float32)).astype(jnp.bfloat16)
        lhs = jnp.concatenate([high, rest], axis=0)
        fan, plain = fan_out(refs_ref[...].astype(jnp.float32), 1)
        total = off[...]
        for c in range(STEP_CYCLES):
            piece = plain[c * ANGLES : (c + 1) * ANGLES]
            total = total + wts[:, c : c + 1] * jnp.sum(piece * piece, axis=0, keepdims=True)
        off[...] = total
        for q in range(COARSE):
            acc[q] += jnp.dot(
                lhs, roll_rows(fan, SHIFT * FINE * q), preferred_element_type=jnp.float32
            )

    @pl.when(step == STEPS - 1)
    def _():
        aux = aux_ref[...]
        live = aux[:, ROTATIONS : ROTATIONS + 1]
        wsum = aux[:, ROTATIONS + 1 : ROTATIONS + 2]
        low = lax.broadcasted_iota(jnp.int32, (owned, half), 1) < owned
        base = -0.5 * off[...]
        strength = str_ref[...]
        top = None
        for q in range(COARSE):
            for t in range(FINE // 2):
                r = q * FINE + 2 * t
                cols = slice(t * half, (t + 1) * half)
                turn = jnp.where(low, aux[:, r : r + 1], aux[:, r + 1 : r + 2])
                score = acc[q, :owned, cols] + acc[q, owned:, cols] + base + turn * strength
                acc[q, :owned, cols] = score
                top = score if top is None else jnp.maximum(top, score)
        top = jnp.max(top, axis=1, keepdims=True)
        norm = jnp.zeros((owned, half), jnp.float32)
        for q in range(COARSE):
            for t in range(FINE // 2):
                cols = slice(t * half, (t + 1) * half)
                term = jnp.exp(acc[q, :owned, cols] - top)
                acc[q, :owned, cols] = term
                norm = norm + term
        norm = jnp.sum(norm, axis=1, keepdims=True)
        ev_ref[...] = jnp.where(live > 0.0, (top + jnp.log(norm)) / (ANGLES * wsum), 0.0)
        seen = jnp.zeros((owned, half), jnp.float32)

        def weight(q, t):
            cols = slice(t * half, (t + 1) * half)
            value = jnp.where(live > 0.0, acc[q, :owned, cols] / norm, 0.0)
            return value.astype(jnp.bfloat16).astype(jnp.float32)

        for q in range(0, COARSE, 2):
            for t in range(FINE // 2):
                first, second = weight(q, t), weight(q + 1, t)
                seen = seen + first + second
                even = jnp.where(low, first, pltpu.roll(second, half // 2, 1))
                odd = jnp.where(low, pltpu.roll(first, half // 2, 1), second)
                cols = slice(q // 2 * half, (q // 2 + 1) * half)
                post[2 * t * owned : (2 * t + 1) * owned, cols] = even.astype(jnp.bfloat16)
                post[(2 * t + 1) * owned : (2 * t + 2) * owned, cols] = odd.astype(jnp.bfloat16)
        seen = jnp.sum(seen, axis=0, keepdims=True)
        mass[...] = seen + pltpu.roll(seen, half // 2, 1)


def turned_sums(boxes, post):
    half = 2 * boxes.shape[0]
    fan, _unused = fan_out(boxes.astype(jnp.float32), -1)
    sums = jnp.dot(fan, post, preferred_element_type=jnp.float32)
    both = sums[:, :half]
    for p in range(1, COARSE // 2):
        both = both + roll_rows(sums[:, p * half : (p + 1) * half], -2 * p * SHIFT * FINE)
    whole = both + pltpu.roll(roll_rows(both, -SHIFT * FINE), half // 2, 1)
    return whole.T


def plain_sums_kernel(width, boxes_ref, post_ref, mass_ref, out_ref):
    turned = turned_sums(boxes_ref[...], post_ref[...])
    classes = out_ref.shape[2]
    mass = jnp.broadcast_to(mass_ref[...], (128, 128)).T
    for h in range(2):
        rows = turned[h * classes : (h + 1) * classes]
        tail = mass[h * classes : (h + 1) * classes, : out_ref.shape[3] - width]
        for j in range(STEP // width):
            out_ref[j, h, :, :width] = rows[:, j * width : (j + 1) * width]
            out_ref[j, h, :, width:] = tail


def plain_sums(boxes, post, mass, classes, peers):
    width = CYCLES // peers * ANGLES
    padded = (width + 1 + 127) // 128 * 128
    return pl.pallas_call(
        functools.partial(plain_sums_kernel, width),
        grid=(STEPS,),
        in_specs=[
            pl.BlockSpec((boxes.shape[0], STEP), lambda i: (0, i)),
            pl.BlockSpec(post.shape, lambda i: (0, 0)),
            pl.BlockSpec(mass.shape, lambda i: (0, 0)),
        ],
        out_specs=pl.BlockSpec((STEP // width, 2, classes, padded), lambda i: (i, 0, 0, 0)),
        out_shape=jax.ShapeDtypeStruct((peers, 2, classes, padded), jnp.float32),
    )(boxes, post, mass)


def scores(boxes, refs, wts, aux, strength):
    owned, classes, half = boxes.shape[0], refs.shape[0], strength.shape[1]
    whole = lambda shape: pl.BlockSpec(shape, lambda i: (0, 0))
    post = (FINE * owned, COARSE * classes)
    return pl.pallas_call(
        score_kernel,
        grid=(STEPS,),
        in_specs=[
            pl.BlockSpec((owned, STEP), lambda i: (0, i)),
            pl.BlockSpec((classes, STEP), lambda i: (0, i)),
            pl.BlockSpec((1, owned, STEP_CYCLES), lambda i: (i, 0, 0)),
            whole(aux.shape),
            whole((1, half)),
        ],
        out_specs=[whole(post), whole((1, half)), whole((owned, 1))],
        out_shape=[
            jax.ShapeDtypeStruct(post, jnp.bfloat16),
            jax.ShapeDtypeStruct((1, half), jnp.float32),
            jax.ShapeDtypeStruct((owned, 1), jnp.float32),
        ],
        scratch_shapes=[
            pltpu.VMEM((COARSE, 2 * owned, FINE * classes), jnp.float32),
            pltpu.VMEM((owned, half), jnp.float32),
        ],
        compiler_params=pltpu.CompilerParams(
            dimension_semantics=("arbitrary",), vmem_limit_bytes=40 * 1024 * 1024
        ),
    )(boxes, refs, wts, aux, strength)


MESH = pl.DeviceIdType.MESH
CHUNKS = 4


def greet(devices):
    barrier = pltpu.get_barrier_semaphore()
    for device in devices:
        pl.semaphore_signal(barrier, inc=1, device_id=device, device_id_type=MESH)
    pl.semaphore_wait(barrier, len(devices))


def gather_kernel(peers, refs_ref, row_ref, all_refs, all_rows, local, send, recv):
    mine, core = lax.axis_index("particle"), lax.axis_index("classes")
    partner = {"classes": 1 - core}
    others = [{"particle": lax.rem(mine + d, peers)} for d in range(1, peers)]
    greet([partner] + others)
    copies = [
        pltpu.make_async_remote_copy(
            src_ref=refs_ref, dst_ref=all_refs.at[core], send_sem=send.at[0], recv_sem=recv.at[0],
            device_id=partner, device_id_type=MESH,
        ),
        pltpu.make_async_remote_copy(
            src_ref=row_ref, dst_ref=all_rows.at[peers], send_sem=send.at[1], recv_sem=recv.at[1],
            device_id=partner, device_id_type=MESH,
        ),
    ]
    for d, other in enumerate(others):
        copies.append(
            pltpu.make_async_remote_copy(
                src_ref=row_ref, dst_ref=all_rows.at[mine], send_sem=send.at[2 + d],
                recv_sem=recv.at[2 + d], device_id=other, device_id_type=MESH,
            )
        )
    for copy in copies:
        copy.start()
    own = [
        pltpu.make_async_copy(refs_ref, all_refs.at[core], local.at[0]),
        pltpu.make_async_copy(row_ref, all_rows.at[mine], local.at[1]),
    ]
    for copy in own:
        copy.start()
    for copy in own + copies:
        copy.wait()


def gathered(refs, row, peers):
    return pl.pallas_call(
        functools.partial(gather_kernel, peers),
        in_specs=[pl.BlockSpec(memory_space=pltpu.VMEM)] * 2,
        out_specs=[pl.BlockSpec(memory_space=pltpu.VMEM)] * 2,
        out_shape=[
            jax.ShapeDtypeStruct((2,) + refs.shape, refs.dtype),
            jax.ShapeDtypeStruct((peers + 1,) + row.shape, row.dtype),
        ],
        scratch_shapes=[
            pltpu.SemaphoreType.DMA((2,)),
            pltpu.SemaphoreType.DMA((peers + 1,)),
            pltpu.SemaphoreType.DMA((peers + 1,)),
        ],
        compiler_params=pltpu.CompilerParams(collective_id=0, has_side_effects=True),
    )(refs, row)


def scatter_kernel(depth, parts, out, pair_in, side_out, side_in, line_out, line_in,
                   pair_send, pair_recv, side_send, side_recv, line_send, line_recv):
    mine, core = lax.axis_index("particle"), lax.axis_index("classes")
    level, side = mine // 2, lax.rem(mine, 2)
    partner = {"classes": 1 - core}
    across = {"particle": level * 2 + 1 - side}
    levels = [lax.rem(level + d, depth) for d in range(1, depth)]
    line = [{"particle": other * 2 + side} for other in levels]
    greet([partner, across] + line)
    rows = out.shape[0] // CHUNKS
    pair, cross, lines = [], [], []
    for j in range(CHUNKS):
        copy = pltpu.make_async_remote_copy(
            src_ref=parts.at[:, :, 1 - core, j * rows : (j + 1) * rows], dst_ref=pair_in.at[j],
            send_sem=pair_send.at[j], recv_sem=pair_recv.at[j], device_id=partner,
            device_id_type=MESH,
        )
        copy.start()
        pair.append(copy)
    for j in range(CHUNKS):
        span = slice(j * rows, (j + 1) * rows)
        pair[j].wait_recv()
        side_out[j] = parts[:, 1 - side, core, span] + pair_in[j, :, 1 - side]
        copy = pltpu.make_async_remote_copy(
            src_ref=side_out.at[j], dst_ref=side_in.at[j], send_sem=side_send.at[j],
            recv_sem=side_recv.at[j], device_id=across, device_id_type=MESH,
        )
        copy.start()
        cross.append(copy)
        line_out[j] = parts[:, side, core, span] + pair_in[j, :, side]
    for j in range(CHUNKS):
        cross[j].wait_recv()
        line_out[j] = line_out[j] + side_in[j]
        for d in range(depth - 1):
            copy = pltpu.make_async_remote_copy(
                src_ref=line_out.at[j, levels[d]], dst_ref=line_in.at[j, d],
                send_sem=line_send.at[j, d], recv_sem=line_recv.at[j, d], device_id=line[d],
                device_id_type=MESH,
            )
            copy.start()
            lines.append(copy)
    for j in range(CHUNKS):
        total = line_out[j, level]
        for d in range(depth - 1):
            lines[j * (depth - 1) + d].wait_recv()
            total = total + line_in[j, d]
        out[j * rows : (j + 1) * rows] = total
    for copy in pair + cross + lines:
        copy.wait_send()


def scattered(parts):
    peers, _, classes, width = parts.shape
    depth = peers // 2
    rows = classes // CHUNKS
    sems = pltpu.SemaphoreType.DMA((CHUNKS,))
    line_sems = pltpu.SemaphoreType.DMA((CHUNKS, max(depth - 1, 1)))
    return pl.pallas_call(
        functools.partial(scatter_kernel, depth),
        in_specs=[pl.BlockSpec(memory_space=pltpu.VMEM)],
        out_specs=pl.BlockSpec(memory_space=pltpu.VMEM),
        out_shape=jax.ShapeDtypeStruct((classes, width), jnp.float32),
        scratch_shapes=[
            pltpu.VMEM((CHUNKS, depth, 2, rows, width), jnp.float32),
            pltpu.VMEM((CHUNKS, depth, rows, width), jnp.float32),
            pltpu.VMEM((CHUNKS, depth, rows, width), jnp.float32),
            pltpu.VMEM((CHUNKS, depth, rows, width), jnp.float32),
            pltpu.VMEM((CHUNKS, max(depth - 1, 1), rows, width), jnp.float32),
            sems, sems, sems, sems, line_sems, line_sems,
        ],
        compiler_params=pltpu.CompilerParams(
            collective_id=1, has_side_effects=True, vmem_limit_bytes=48 * 1024 * 1024
        ),
    )(parts.reshape(depth, 2, 2, classes, width))


def sums_kernel(peers, boxes, post, mass, refs, out, pair_out, pair_in, keep, side_out, side_in,
                line_in, mass_in, column, pair_send, pair_recv, side_send, side_recv, line_send,
                line_recv, mass_send, mass_recv):
    mine, core = lax.axis_index("particle"), lax.axis_index("classes")
    depth, width, classes = peers // 2, out.shape[1], out.shape[0]
    level, side = mine // 2, lax.rem(mine, 2)
    place = mine * 2 + core
    partner = {"classes": 1 - core}
    across = {"particle": level * 2 + 1 - side}
    everyone = []
    for e in range(1, 2 * peers):
        there = lax.rem(place + e, 2 * peers)
        everyone.append({"particle": there // 2, "classes": lax.rem(there, 2)})
    greet(everyone)
    started, masses = [], []

    def send(src, dst, sends, recvs, device):
        copy = pltpu.make_async_remote_copy(
            src_ref=src, dst_ref=dst, send_sem=sends, recv_sem=recvs, device_id=device,
            device_id_type=MESH,
        )
        copy.start()
        started.append(copy)
        return copy

    for e, device in enumerate(everyone):
        masses.append(
            send(mass, mass_in.at[e], mass_send.at[e], mass_recv.at[e], device)
        )
    turns = list(range(1, depth)) + [0]
    blocks = [(i, d, True) for i, d in enumerate(turns)] + [(i, d, False) for i, d in enumerate(turns)]
    pair, cross, lines = [], [], []

    def advance(n):
        i, d, away = blocks[n]
        pair[n].wait_recv()
        if away:
            side_out[i] = keep[n] + pair_in[n]
            cross.append(
                send(side_out.at[i], side_in.at[i], side_send.at[i], side_recv.at[i], across)
            )
            return
        cross[i].wait_recv()
        keep[n] = keep[n] + pair_in[n] + side_in[i]
        if d > 0:
            there = {"particle": lax.rem(level + d, depth) * 2 + side}
            lines.append(
                send(keep.at[n], line_in.at[i], line_send.at[i], line_recv.at[i], there)
            )

    for n, (i, d, away) in enumerate(blocks):
        shard = lax.rem(level + d, depth) * 2 + (1 - side if away else side)

        @pl.loop(0, width // STEP)
        def _(part):
            source = pl.multiple_of(shard * width + part * STEP, 128)
            target = pl.multiple_of(part * STEP, 128)
            turned = turned_sums(boxes[:, pl.ds(source, STEP)], post[...])
            low, high = turned[:classes], turned[classes : 2 * classes]
            keep[n, :, pl.ds(target, STEP)] = jnp.where(core == 0, low, high)
            pair_out[n, :, pl.ds(target, STEP)] = jnp.where(core == 0, high, low)

        pair.append(send(pair_out.at[n], pair_in.at[n], pair_send.at[n], pair_recv.at[n], partner))
        if n > 0:
            advance(n - 1)
    advance(len(blocks) - 1)
    weight = mass[...]
    for e, copy in enumerate(masses):
        copy.wait_recv()
        weight = weight + mass_in[e]
    column[...] = jnp.broadcast_to(weight, column.shape).T
    scale = column[pl.ds(pl.multiple_of(core * classes, 8), classes), :]
    total = keep[len(blocks) - 1]
    for i in range(depth - 1):
        lines[i].wait_recv()
        total = total + line_in[i]
    base = refs[:, pl.ds(pl.multiple_of(mine * width, 128), width)].astype(jnp.float32)
    out[...] = (total + base) / (scale[:, 0:1] + 1.0)
    for copy in started:
        copy.wait_send()


def fused_sums(boxes, post, mass, refs, peers):
    classes, width, depth = refs.shape[0], CYCLES // peers * ANGLES, peers // 2
    room = lambda count: pltpu.VMEM((count, classes, width), jnp.float32)
    sems = lambda count: pltpu.SemaphoreType.DMA((count,))
    others = 2 * peers - 1
    return pl.pallas_call(
        functools.partial(sums_kernel, peers),
        in_specs=[pl.BlockSpec(memory_space=pltpu.VMEM)] * 4,
        out_specs=pl.BlockSpec(memory_space=pltpu.VMEM),
        out_shape=jax.ShapeDtypeStruct((classes, width), jnp.float32),
        scratch_shapes=[
            room(peers), room(peers), room(peers), room(depth), room(depth), room(depth - 1),
            pltpu.VMEM((others,) + mass.shape, jnp.float32),
            pltpu.VMEM((mass.shape[1], mass.shape[1]), jnp.float32),
            sems(peers), sems(peers), sems(depth), sems(depth), sems(depth - 1), sems(depth - 1),
            sems(others), sems(others),
        ],
        compiler_params=pltpu.CompilerParams(
            collective_id=2, has_side_effects=True, vmem_limit_bytes=48 * 1024 * 1024
        ),
    )(boxes, post, mass, refs)


def on_device(boxes, counts, destinations, prior_rot, references, cycle_weights, prior_strength):
    peers = lax.axis_size("particle")
    cycle_index = lax.axis_index("particle")
    cycles_dev = CYCLES // peers
    width = cycles_dev * ANGLES
    owned = boxes.shape[0]
    classes_dev = references.shape[0]
    lane_index = lax.axis_index("classes")
    row = jnp.concatenate([cycle_weights[0], prior_strength])
    row = jnp.pad(row, (0, 128 - row.shape[0]))[None, :]
    refs, rows = gathered(references, row, peers)
    refs = refs.reshape(2 * classes_dev, -1)
    group_wts = rows[:peers, 0, :CYCLES]
    other = rows[peers, 0, CYCLES : CYCLES + classes_dev]
    strength = jnp.where(
        lane_index == 0,
        jnp.concatenate([prior_strength, other]),
        jnp.concatenate([other, prior_strength]),
    ).reshape(1, -1)
    mine = destinations[:, None] == jnp.arange(peers, dtype=jnp.int32)[None, :]
    wts = jnp.sum(jnp.where(mine[:, :, None], group_wts[None], 0.0), axis=1)
    live = (jnp.arange(owned, dtype=jnp.int32) < counts[0]).astype(jnp.float32)
    turn_ids = jnp.arange(ROTATIONS, dtype=jnp.float32)
    gap = TWO_PI * (turn_ids[None, :] - prior_rot[:, None].astype(jnp.float32)) / ROTATIONS
    aux = jnp.concatenate([jnp.cos(gap), live[:, None], jnp.sum(wts, axis=1)[:, None]], axis=1)
    wts = jnp.transpose(wts.reshape(owned, STEPS, STEP_CYCLES), (1, 0, 2))
    post, mass, evidence = scores(
        boxes, refs, wts, aux, jnp.concatenate([strength, strength], axis=1)
    )
    if width % STEP == 0:
        new_references = fused_sums(boxes, post, mass, references, peers)
    else:
        sums = scattered(plain_sums(boxes, post, mass, classes_dev, peers))
        own_refs = lax.dynamic_slice_in_dim(references, cycle_index * width, width, 1)
        new_references = (sums[:, :width] + own_refs.astype(jnp.float32)) / (
            sums[:, width : width + 1] + 1.0
        )
    return new_references.reshape(classes_dev, cycles_dev, ANGLES), evidence[:, 0]


def solution(mesh):
    in_specs = (
        P(("groups", "particle", "classes"), None),
        P(("groups", "particle", "classes")),
        P(("groups", "particle", "classes")),
        P(("groups", "particle", "classes")),
        P(("groups", "classes"), None),
        P(("groups", "particle"), None),
        P(("groups", "classes")),
    )
    out_specs = (P(("groups", "classes"), "particle", None), P(("groups", "particle", "classes")))
    return jax.shard_map(
        on_device, mesh=mesh, in_specs=in_specs, out_specs=out_specs, check_vma=False
    )
```

```python
import functools
import math

import jax
import jax.numpy as jnp
from jax import lax
from jax.experimental import pallas as pl
from jax.experimental.pallas import tpu as pltpu
from jax.sharding import PartitionSpec as P

CYCLES = 64
ANGLES = 192
ROTATIONS = 24
FINE = 4
COARSE = ROTATIONS // FINE
SHIFT = ANGLES // ROTATIONS
STEP_CYCLES = 4
STEP = STEP_CYCLES * ANGLES
STEPS = CYCLES // STEP_CYCLES
TWO_PI = 2.0 * math.pi


def roll_rows(block, shift):
    shift = shift % ANGLES
    if shift == 0:
        return block
    pieces = []
    for c in range(STEP_CYCLES):
        base = c * ANGLES
        pieces.append(block[base + ANGLES - shift : base + ANGLES])
        pieces.append(block[base : base + ANGLES - shift])
    return jnp.concatenate(pieces, axis=0)


def fan_out(rows, sign):
    plain = jnp.concatenate([rows, rows], axis=0).T
    low = lax.broadcasted_iota(jnp.int32, plain.shape, 1) < rows.shape[0]
    tiles = [
        jnp.where(low, roll_rows(plain, sign * SHIFT * f), roll_rows(plain, sign * SHIFT * (f + 1)))
        for f in range(0, FINE, 2)
    ]
    return jnp.concatenate([t.astype(jnp.bfloat16) for t in tiles], axis=1), plain


def score_kernel(boxes_ref, refs_ref, wts_ref, aux_ref, str_ref, post, mass, ev_ref, acc, off):
    step = pl.program_id(0)
    owned = boxes_ref.shape[0]
    half = str_ref.shape[1]

    @pl.when(step == 0)
    def _():
        acc[...] = jnp.zeros_like(acc)
        off[...] = jnp.zeros_like(off)

    @pl.when(step >= 0)
    def _():
        wts = wts_ref[0]
        lane = lax.broadcasted_iota(jnp.int32, (owned, STEP), 1)
        spread = jnp.broadcast_to(wts[:, 0:1], (owned, STEP))
        for c in range(1, STEP_CYCLES):
            spread = jnp.where(lane >= c * ANGLES, wts[:, c : c + 1], spread)
        scaled = boxes_ref[...].astype(jnp.float32) * spread
        high = scaled.astype(jnp.bfloat16)
        rest = (scaled - high.astype(jnp.float32)).astype(jnp.bfloat16)
        lhs = jnp.concatenate([high, rest], axis=0)
        fan, plain = fan_out(refs_ref[...].astype(jnp.float32), 1)
        total = off[...]
        for c in range(STEP_CYCLES):
            piece = plain[c * ANGLES : (c + 1) * ANGLES]
            total = total + wts[:, c : c + 1] * jnp.sum(piece * piece, axis=0, keepdims=True)
        off[...] = total
        for q in range(COARSE):
            acc[q] += jnp.dot(
                lhs, roll_rows(fan, SHIFT * FINE * q), preferred_element_type=jnp.float32
            )

    @pl.when(step == STEPS - 1)
    def _():
        aux = aux_ref[...]
        live = aux[:, ROTATIONS : ROTATIONS + 1]
        wsum = aux[:, ROTATIONS + 1 : ROTATIONS + 2]
        low = lax.broadcasted_iota(jnp.int32, (owned, half), 1) < owned
        base = -0.5 * off[...]
        strength = str_ref[...]
        top = None
        for q in range(COARSE):
            for t in range(FINE // 2):
                r = q * FINE + 2 * t
                cols = slice(t * half, (t + 1) * half)
                turn = jnp.where(low, aux[:, r : r + 1], aux[:, r + 1 : r + 2])
                score = acc[q, :owned, cols] + acc[q, owned:, cols] + base + turn * strength
                acc[q, :owned, cols] = score
                top = score if top is None else jnp.maximum(top, score)
        top = jnp.max(top, axis=1, keepdims=True)
        norm = jnp.zeros((owned, half), jnp.float32)
        for q in range(COARSE):
            for t in range(FINE // 2):
                cols = slice(t * half, (t + 1) * half)
                term = jnp.exp(acc[q, :owned, cols] - top)
                acc[q, :owned, cols] = term
                norm = norm + term
        norm = jnp.sum(norm, axis=1, keepdims=True)
        ev_ref[...] = jnp.where(live > 0.0, (top + jnp.log(norm)) / (ANGLES * wsum), 0.0)
        seen = jnp.zeros((owned, half), jnp.float32)

        def weight(q, t):
            cols = slice(t * half, (t + 1) * half)
            value = jnp.where(live > 0.0, acc[q, :owned, cols] / norm, 0.0)
            return value.astype(jnp.bfloat16).astype(jnp.float32)

        for q in range(0, COARSE, 2):
            for t in range(FINE // 2):
                first, second = weight(q, t), weight(q + 1, t)
                seen = seen + first + second
                even = jnp.where(low, first, pltpu.roll(second, half // 2, 1))
                odd = jnp.where(low, pltpu.roll(first, half // 2, 1), second)
                cols = slice(q // 2 * half, (q // 2 + 1) * half)
                post[2 * t * owned : (2 * t + 1) * owned, cols] = even.astype(jnp.bfloat16)
                post[(2 * t + 1) * owned : (2 * t + 2) * owned, cols] = odd.astype(jnp.bfloat16)
        seen = jnp.sum(seen, axis=0, keepdims=True)
        mass[...] = seen + pltpu.roll(seen, half // 2, 1)


def turned_sums(boxes, post):
    half = 2 * boxes.shape[0]
    fan, _unused = fan_out(boxes.astype(jnp.float32), -1)
    sums = jnp.dot(fan, post, preferred_element_type=jnp.float32)
    both = sums[:, :half]
    for p in range(1, COARSE // 2):
        both = both + roll_rows(sums[:, p * half : (p + 1) * half], -2 * p * SHIFT * FINE)
    whole = both + pltpu.roll(roll_rows(both, -SHIFT * FINE), half // 2, 1)
    return whole.T


def plain_sums_kernel(width, boxes_ref, post_ref, mass_ref, out_ref):
    turned = turned_sums(boxes_ref[...], post_ref[...])
    classes = out_ref.shape[2]
    mass = jnp.broadcast_to(mass_ref[...], (128, 128)).T
    for h in range(2):
        rows = turned[h * classes : (h + 1) * classes]
        tail = mass[h * classes : (h + 1) * classes, : out_ref.shape[3] - width]
        for j in range(STEP // width):
            out_ref[j, h, :, :width] = rows[:, j * width : (j + 1) * width]
            out_ref[j, h, :, width:] = tail


def plain_sums(boxes, post, mass, classes, peers):
    width = CYCLES // peers * ANGLES
    padded = (width + 1 + 127) // 128 * 128
    return pl.pallas_call(
        functools.partial(plain_sums_kernel, width),
        grid=(STEPS,),
        in_specs=[
            pl.BlockSpec((boxes.shape[0], STEP), lambda i: (0, i)),
            pl.BlockSpec(post.shape, lambda i: (0, 0)),
            pl.BlockSpec(mass.shape, lambda i: (0, 0)),
        ],
        out_specs=pl.BlockSpec((STEP // width, 2, classes, padded), lambda i: (i, 0, 0, 0)),
        out_shape=jax.ShapeDtypeStruct((peers, 2, classes, padded), jnp.float32),
    )(boxes, post, mass)


def scores(boxes, refs, wts, aux, strength):
    owned, classes, half = boxes.shape[0], refs.shape[0], strength.shape[1]
    whole = lambda shape: pl.BlockSpec(shape, lambda i: (0, 0))
    post = (FINE * owned, COARSE * classes)
    return pl.pallas_call(
        score_kernel,
        grid=(STEPS,),
        in_specs=[
            pl.BlockSpec((owned, STEP), lambda i: (0, i)),
            pl.BlockSpec((classes, STEP), lambda i: (0, i)),
            pl.BlockSpec((1, owned, STEP_CYCLES), lambda i: (i, 0, 0)),
            whole(aux.shape),
            whole((1, half)),
        ],
        out_specs=[whole(post), whole((1, half)), whole((owned, 1))],
        out_shape=[
            jax.ShapeDtypeStruct(post, jnp.bfloat16),
            jax.ShapeDtypeStruct((1, half), jnp.float32),
            jax.ShapeDtypeStruct((owned, 1), jnp.float32),
        ],
        scratch_shapes=[
            pltpu.VMEM((COARSE, 2 * owned, FINE * classes), jnp.float32),
            pltpu.VMEM((owned, half), jnp.float32),
        ],
        compiler_params=pltpu.CompilerParams(
            dimension_semantics=("arbitrary",), vmem_limit_bytes=40 * 1024 * 1024
        ),
    )(boxes, refs, wts, aux, strength)


MESH = pl.DeviceIdType.MESH
CHUNKS = 4


def greet(devices):
    barrier = pltpu.get_barrier_semaphore()
    for device in devices:
        pl.semaphore_signal(barrier, inc=1, device_id=device, device_id_type=MESH)
    pl.semaphore_wait(barrier, len(devices))


def gather_kernel(peers, refs_ref, row_ref, all_refs, all_rows, local, send, recv):
    mine, core = lax.axis_index("particle"), lax.axis_index("classes")
    partner = {"classes": 1 - core}
    others = [{"particle": lax.rem(mine + d, peers)} for d in range(1, peers)]
    greet([partner] + others)
    copies = [
        pltpu.make_async_remote_copy(
            src_ref=refs_ref, dst_ref=all_refs.at[core], send_sem=send.at[0], recv_sem=recv.at[0],
            device_id=partner, device_id_type=MESH,
        ),
        pltpu.make_async_remote_copy(
            src_ref=row_ref, dst_ref=all_rows.at[peers], send_sem=send.at[1], recv_sem=recv.at[1],
            device_id=partner, device_id_type=MESH,
        ),
    ]
    for d, other in enumerate(others):
        copies.append(
            pltpu.make_async_remote_copy(
                src_ref=row_ref, dst_ref=all_rows.at[mine], send_sem=send.at[2 + d],
                recv_sem=recv.at[2 + d], device_id=other, device_id_type=MESH,
            )
        )
    for copy in copies:
        copy.start()
    own = [
        pltpu.make_async_copy(refs_ref, all_refs.at[core], local.at[0]),
        pltpu.make_async_copy(row_ref, all_rows.at[mine], local.at[1]),
    ]
    for copy in own:
        copy.start()
    for copy in own + copies:
        copy.wait()


def gathered(refs, row, peers):
    return pl.pallas_call(
        functools.partial(gather_kernel, peers),
        in_specs=[pl.BlockSpec(memory_space=pltpu.VMEM)] * 2,
        out_specs=[pl.BlockSpec(memory_space=pltpu.VMEM)] * 2,
        out_shape=[
            jax.ShapeDtypeStruct((2,) + refs.shape, refs.dtype),
            jax.ShapeDtypeStruct((peers + 1,) + row.shape, row.dtype),
        ],
        scratch_shapes=[
            pltpu.SemaphoreType.DMA((2,)),
            pltpu.SemaphoreType.DMA((peers + 1,)),
            pltpu.SemaphoreType.DMA((peers + 1,)),
        ],
        compiler_params=pltpu.CompilerParams(collective_id=0, has_side_effects=True),
    )(refs, row)


def scatter_kernel(depth, parts, out, pair_in, side_out, side_in, line_out, line_in,
                   pair_send, pair_recv, side_send, side_recv, line_send, line_recv):
    mine, core = lax.axis_index("particle"), lax.axis_index("classes")
    level, side = mine // 2, lax.rem(mine, 2)
    partner = {"classes": 1 - core}
    across = {"particle": level * 2 + 1 - side}
    levels = [lax.rem(level + d, depth) for d in range(1, depth)]
    line = [{"particle": other * 2 + side} for other in levels]
    greet([partner, across] + line)
    rows = out.shape[0] // CHUNKS
    pair, cross, lines = [], [], []
    for j in range(CHUNKS):
        copy = pltpu.make_async_remote_copy(
            src_ref=parts.at[:, :, 1 - core, j * rows : (j + 1) * rows], dst_ref=pair_in.at[j],
            send_sem=pair_send.at[j], recv_sem=pair_recv.at[j], device_id=partner,
            device_id_type=MESH,
        )
        copy.start()
        pair.append(copy)
    for j in range(CHUNKS):
        span = slice(j * rows, (j + 1) * rows)
        pair[j].wait_recv()
        side_out[j] = parts[:, 1 - side, core, span] + pair_in[j, :, 1 - side]
        copy = pltpu.make_async_remote_copy(
            src_ref=side_out.at[j], dst_ref=side_in.at[j], send_sem=side_send.at[j],
            recv_sem=side_recv.at[j], device_id=across, device_id_type=MESH,
        )
        copy.start()
        cross.append(copy)
        line_out[j] = parts[:, side, core, span] + pair_in[j, :, side]
    for j in range(CHUNKS):
        cross[j].wait_recv()
        line_out[j] = line_out[j] + side_in[j]
        for d in range(depth - 1):
            copy = pltpu.make_async_remote_copy(
                src_ref=line_out.at[j, levels[d]], dst_ref=line_in.at[j, d],
                send_sem=line_send.at[j, d], recv_sem=line_recv.at[j, d], device_id=line[d],
                device_id_type=MESH,
            )
            copy.start()
            lines.append(copy)
    for j in range(CHUNKS):
        total = line_out[j, level]
        for d in range(depth - 1):
            lines[j * (depth - 1) + d].wait_recv()
            total = total + line_in[j, d]
        out[j * rows : (j + 1) * rows] = total
    for copy in pair + cross + lines:
        copy.wait_send()


def scattered(parts):
    peers, _, classes, width = parts.shape
    depth = peers // 2
    rows = classes // CHUNKS
    sems = pltpu.SemaphoreType.DMA((CHUNKS,))
    line_sems = pltpu.SemaphoreType.DMA((CHUNKS, max(depth - 1, 1)))
    return pl.pallas_call(
        functools.partial(scatter_kernel, depth),
        in_specs=[pl.BlockSpec(memory_space=pltpu.VMEM)],
        out_specs=pl.BlockSpec(memory_space=pltpu.VMEM),
        out_shape=jax.ShapeDtypeStruct((classes, width), jnp.float32),
        scratch_shapes=[
            pltpu.VMEM((CHUNKS, depth, 2, rows, width), jnp.float32),
            pltpu.VMEM((CHUNKS, depth, rows, width), jnp.float32),
            pltpu.VMEM((CHUNKS, depth, rows, width), jnp.float32),
            pltpu.VMEM((CHUNKS, depth, rows, width), jnp.float32),
            pltpu.VMEM((CHUNKS, max(depth - 1, 1), rows, width), jnp.float32),
            sems, sems, sems, sems, line_sems, line_sems,
        ],
        compiler_params=pltpu.CompilerParams(
            collective_id=1, has_side_effects=True, vmem_limit_bytes=48 * 1024 * 1024
        ),
    )(parts.reshape(depth, 2, 2, classes, width))


def sums_kernel(peers, boxes, post, mass, refs, out, pair_out, pair_in, keep, side_out, side_in,
                line_in, mass_in, column, pair_send, pair_recv, side_send, side_recv, line_send,
                line_recv, mass_send, mass_recv):
    mine, core = lax.axis_index("particle"), lax.axis_index("classes")
    depth, width, classes = peers // 2, out.shape[1], out.shape[0]
    level, side = mine // 2, lax.rem(mine, 2)
    place = mine * 2 + core
    partner = {"classes": 1 - core}
    across = {"particle": level * 2 + 1 - side}
    everyone = []
    for e in range(1, 2 * peers):
        there = lax.rem(place + e, 2 * peers)
        everyone.append({"particle": there // 2, "classes": lax.rem(there, 2)})
    greet(everyone)
    started, masses = [], []

    def send(src, dst, sends, recvs, device):
        copy = pltpu.make_async_remote_copy(
            src_ref=src, dst_ref=dst, send_sem=sends, recv_sem=recvs, device_id=device,
            device_id_type=MESH,
        )
        copy.start()
        started.append(copy)
        return copy

    for e, device in enumerate(everyone):
        masses.append(
            send(mass, mass_in.at[e], mass_send.at[e], mass_recv.at[e], device)
        )
    turns = sorted(range(1, depth), key=lambda d: -min(d, depth - d)) + [0]
    blocks = [(i, d, True) for i, d in enumerate(turns)] + [(i, d, False) for i, d in enumerate(turns)]
    pair, cross, lines = [], [], []

    def advance(n):
        i, d, away = blocks[n]
        pair[n].wait_recv()
        if away:
            side_out[i] = keep[n] + pair_in[n]
            cross.append(
                send(side_out.at[i], side_in.at[i], side_send.at[i], side_recv.at[i], across)
            )
            return
        cross[i].wait_recv()
        keep[n] = keep[n] + pair_in[n] + side_in[i]
        if d > 0:
            there = {"particle": lax.rem(level + d, depth) * 2 + side}
            lines.append(
                send(keep.at[n], line_in.at[i], line_send.at[i], line_recv.at[i], there)
            )

    for n, (i, d, away) in enumerate(blocks):
        shard = lax.rem(level + d, depth) * 2 + (1 - side if away else side)

        @pl.loop(0, width // STEP)
        def _(part):
            source = pl.multiple_of(shard * width + part * STEP, 128)
            target = pl.multiple_of(part * STEP, 128)
            turned = turned_sums(boxes[:, pl.ds(source, STEP)], post[...])
            low, high = turned[:classes], turned[classes : 2 * classes]
            keep[n, :, pl.ds(target, STEP)] = jnp.where(core == 0, low, high)
            pair_out[n, :, pl.ds(target, STEP)] = jnp.where(core == 0, high, low)

        pair.append(send(pair_out.at[n], pair_in.at[n], pair_send.at[n], pair_recv.at[n], partner))
        if n > 0:
            advance(n - 1)
    advance(len(blocks) - 1)
    weight = mass[...]
    for e, copy in enumerate(masses):
        copy.wait_recv()
        weight = weight + mass_in[e]
    column[...] = jnp.broadcast_to(weight, column.shape).T
    scale = column[pl.ds(pl.multiple_of(core * classes, 8), classes), :]
    total = keep[len(blocks) - 1]
    for i in range(depth - 1):
        lines[i].wait_recv()
        total = total + line_in[i]
    base = refs[:, pl.ds(pl.multiple_of(mine * width, 128), width)].astype(jnp.float32)
    out[...] = (total + base) / (scale[:, 0:1] + 1.0)
    for copy in started:
        copy.wait_send()


def fused_sums(boxes, post, mass, refs, peers):
    classes, width, depth = refs.shape[0], CYCLES // peers * ANGLES, peers // 2
    room = lambda count: pltpu.VMEM((count, classes, width), jnp.float32)
    sems = lambda count: pltpu.SemaphoreType.DMA((count,))
    others = 2 * peers - 1
    return pl.pallas_call(
        functools.partial(sums_kernel, peers),
        in_specs=[pl.BlockSpec(memory_space=pltpu.VMEM)] * 4,
        out_specs=pl.BlockSpec(memory_space=pltpu.VMEM),
        out_shape=jax.ShapeDtypeStruct((classes, width), jnp.float32),
        scratch_shapes=[
            room(peers), room(peers), room(peers), room(depth), room(depth), room(depth - 1),
            pltpu.VMEM((others,) + mass.shape, jnp.float32),
            pltpu.VMEM((mass.shape[1], mass.shape[1]), jnp.float32),
            sems(peers), sems(peers), sems(depth), sems(depth), sems(depth - 1), sems(depth - 1),
            sems(others), sems(others),
        ],
        compiler_params=pltpu.CompilerParams(
            collective_id=2, has_side_effects=True, vmem_limit_bytes=48 * 1024 * 1024
        ),
    )(boxes, post, mass, refs)


def on_device(boxes, counts, destinations, prior_rot, references, cycle_weights, prior_strength):
    peers = lax.axis_size("particle")
    cycle_index = lax.axis_index("particle")
    cycles_dev = CYCLES // peers
    width = cycles_dev * ANGLES
    owned = boxes.shape[0]
    classes_dev = references.shape[0]
    lane_index = lax.axis_index("classes")
    row = jnp.concatenate([cycle_weights[0], prior_strength])
    row = jnp.pad(row, (0, 128 - row.shape[0]))[None, :]
    refs, rows = gathered(references, row, peers)
    refs = refs.reshape(2 * classes_dev, -1)
    group_wts = rows[:peers, 0, :CYCLES]
    other = rows[peers, 0, CYCLES : CYCLES + classes_dev]
    strength = jnp.where(
        lane_index == 0,
        jnp.concatenate([prior_strength, other]),
        jnp.concatenate([other, prior_strength]),
    ).reshape(1, -1)
    mine = destinations[:, None] == jnp.arange(peers, dtype=jnp.int32)[None, :]
    wts = jnp.sum(jnp.where(mine[:, :, None], group_wts[None], 0.0), axis=1)
    live = (jnp.arange(owned, dtype=jnp.int32) < counts[0]).astype(jnp.float32)
    turn_ids = jnp.arange(ROTATIONS, dtype=jnp.float32)
    gap = TWO_PI * (turn_ids[None, :] - prior_rot[:, None].astype(jnp.float32)) / ROTATIONS
    aux = jnp.concatenate([jnp.cos(gap), live[:, None], jnp.sum(wts, axis=1)[:, None]], axis=1)
    wts = jnp.transpose(wts.reshape(owned, STEPS, STEP_CYCLES), (1, 0, 2))
    post, mass, evidence = scores(
        boxes, refs, wts, aux, jnp.concatenate([strength, strength], axis=1)
    )
    if width % STEP == 0:
        new_references = fused_sums(boxes, post, mass, references, peers)
    else:
        sums = scattered(plain_sums(boxes, post, mass, classes_dev, peers))
        own_refs = lax.dynamic_slice_in_dim(references, cycle_index * width, width, 1)
        new_references = (sums[:, :width] + own_refs.astype(jnp.float32)) / (
            sums[:, width : width + 1] + 1.0
        )
    return new_references.reshape(classes_dev, cycles_dev, ANGLES), evidence[:, 0]


def solution(mesh):
    in_specs = (
        P(("groups", "particle", "classes"), None),
        P(("groups", "particle", "classes")),
        P(("groups", "particle", "classes")),
        P(("groups", "particle", "classes")),
        P(("groups", "classes"), None),
        P(("groups", "particle"), None),
        P(("groups", "classes")),
    )
    out_specs = (P(("groups", "classes"), "particle", None), P(("groups", "particle", "classes")))
    return jax.shard_map(
        on_device, mesh=mesh, in_specs=in_specs, out_specs=out_specs, check_vma=False
    )
```
